32 devices in a mesh: wide: 8 (over y, x, core), narrow: 4 (over z).
Axes of the slice: x: 2, y: 2, z: 4, core: 2. Of those that a mesh axis runs over, the one named last changes fastest.
Arguments:
- latent: float32 [2, 64, 256, 512], P(None, 'wide', 'narrow'), may hold values from -6 to 6
- context: bfloat16 [2, 32, 128, 256], P(None, 'wide', 'narrow'), may hold values from -6 to 6
- conv_weight: bfloat16 [3, 3, 256, 512], replicated, may hold values from -0.125 to 0.125
- window_qkv: bfloat16 [512, 1536], replicated, may hold values from -0.25 to 0.25
- window_out: bfloat16 [512, 512], replicated, may hold values from -0.25 to 0.25
- window_bias: float32 [16, 15, 15], replicated, may hold values from -9 to 320
- grid_qkv: bfloat16 [512, 1536], replicated, may hold values from -0.25 to 0.25
- grid_out: bfloat16 [512, 512], replicated, may hold values from -0.25 to 0.25
- grid_bias: float32 [16, 15, 15], replicated, may hold values from -9 to 320
- mlp_gain: float32 [512], replicated, may hold values from 0.1 to 1.9
- mlp_in: bfloat16 [512, 2048], replicated, may hold values from -0.25 to 0.25
- mlp_out: bfloat16 [2048, 512], replicated, may hold values from -0.125 to 0.125
Outputs:
- forecast: float32 [2, 64, 256, 512], P(None, 'wide', 'narrow')
The draws below stay inside these ranges and needn't reach their ends.
All inputs are finite; a program needn't handle non-finite values.
Results may differ from the reference program's by a relative error of at most 0.0055.
Values may be sent and summed in bfloat16 or wider, within the bound.
No kernel may reach another device: no remote copies, remote signals or barrier semaphores. Data moves between devices by JAX's collectives and lax.ppermute only.
A program may use at most 128 MiB of HBM per device.

```python
import jax
import jax.numpy as jnp
from jax import lax

C = 512
HEAD = 32
HEADS = 16
FFN = 2048
CC = 256
WIN = 8
BATCH = 2
H = 64
W = 256


def bias_entries(key):
    span_count = 2 * WIN - 1
    entries = 1.5 * jax.random.normal(key, (HEADS, span_count, span_count), jnp.float32)
    entries = jnp.clip(entries, -9.0, 9.0)
    return entries


def draw_window_bias(key, part):
    return bias_entries(jax.random.fold_in(key, 17))


def draw_grid_bias(key, part):
    return bias_entries(jax.random.fold_in(key, 29))


def block_scale(stream_key, shape, cuts, least, largest):
    factor_of, own = 1.0, jax.random.fold_in(stream_key, 6)
    for dim, parts in cuts:
        draws = jnp.exp(jax.random.uniform(jax.random.fold_in(own, dim), (parts,), jnp.float32, least / len(cuts), largest / len(cuts)))
        factor_of = factor_of * jnp.repeat(draws, shape[dim] // parts).reshape([-1 if axis == dim else 1 for axis in range(len(shape))])
    return factor_of


def centred(key, shape, deviation, limit, shards=(), kind=jnp.bfloat16):
    values = jax.random.normal(key, shape, jnp.float32) * deviation
    if len(shards) > 0:
        values = block_scale(key, shape, shards, -0.22, 0.18) * values
    return jnp.clip(values, min=-limit, max=limit).astype(kind)


def setup_inputs(seed: int = 0) -> dict:
    splits = jax.random.split(jax.random.key(seed), 13)
    return {
        "latent": centred(splits[0], (BATCH, H, W, C), 1.0, 6.0, ((1, 8), (2, 4)), jnp.float32),
        "context": centred(splits[1], (BATCH, H // 2, W // 2, CC), 1.0, 6.0, ((1, 8), (2, 4))),
        "conv_weight": centred(splits[2], (3, 3, CC, C), (9 * CC) ** -0.5, 0.125),
        "window_qkv": centred(splits[3], (C, 3 * C), C ** -0.5, 0.25),
        "window_out": centred(splits[4], (C, C), C ** -0.5, 0.25),
        "window_bias": draw_window_bias(jax.random.fold_in(splits[12], 71), 0),
        "grid_qkv": centred(splits[6], (C, 3 * C), C ** -0.5, 0.25),
        "grid_out": centred(splits[7], (C, C), C ** -0.5, 0.25),
        "grid_bias": draw_grid_bias(jax.random.fold_in(splits[12], 71), 0),
        "mlp_gain": jnp.clip(1.0 + 0.18 * jax.random.normal(splits[9], (C,), jnp.float32), 0.1, 1.9),
        "mlp_in": centred(splits[10], (C, FFN), C ** -0.5, 0.25),
        "mlp_out": centred(splits[11], (FFN, C), FFN ** -0.5, 0.125),
    }


NORM_EPS = 1e-05

def layer_norm(values):
    center = values - lax.optimization_barrier(jnp.mean(values, axis=-1, keepdims=True))
    spread = lax.optimization_barrier(jnp.mean(center * center, axis=-1, keepdims=True))
    return center * lax.rsqrt(spread + NORM_EPS)

def bias_lookup(bias_table):
    span_count = bias_table.shape[1]
    side_count = (span_count + 1) // 2
    places = jnp.arange(side_count * side_count, dtype=jnp.int32)
    row_of = places // side_count
    col_of = places % side_count
    row_step = row_of[:, None] - row_of[None, :] + side_count - 1
    col_step = col_of[:, None] - col_of[None, :] + side_count - 1
    return bias_table[:, row_step, col_step]

def project(values, weight):
    flat = values.reshape(-1, values.shape[-1])
    result = jnp.dot(flat, weight, preferred_element_type=jnp.float32)
    return result.reshape(values.shape[:-1] + (weight.shape[1],))

def upsample(padded, along):
    cell_count = padded.shape[along] - 2
    lower_rows = lax.slice_in_dim(padded, 0, cell_count, axis=along)
    middle = lax.slice_in_dim(padded, 1, cell_count + 1, axis=along)
    even_terms = 0.25 * lower_rows + 0.75 * middle
    upper_rows = lax.slice_in_dim(padded, 2, cell_count + 2, axis=along)
    odd_terms = 0.75 * middle + 0.25 * upper_rows
    paired = jnp.stack([even_terms, odd_terms], axis=along + 1)
    merged_shape = list(even_terms.shape)
    merged_shape[along] = 2 * cell_count
    return paired.reshape(merged_shape)

def to_windows(tiles, side_count):
    samples, row_count, col_count, channels = tiles.shape
    unfolded = tiles.reshape(samples, row_count // side_count, side_count, col_count // side_count, side_count, channels)
    return unfolded.transpose(0, 1, 3, 2, 4, 5).reshape(-1, side_count * side_count, channels)

def from_windows(grouped, samples, row_count, col_count, side_count):
    channels = grouped.shape[-1]
    unfolded = grouped.reshape(samples, row_count // side_count, col_count // side_count, side_count, side_count, channels)
    return unfolded.transpose(0, 1, 3, 2, 4, 5).reshape(samples, row_count, col_count, channels)

def to_grid(tiles, side_count):
    samples, row_count, col_count, channels = tiles.shape
    unfolded = tiles.reshape(samples, side_count, row_count // side_count, side_count, col_count // side_count, channels)
    return unfolded.transpose(0, 2, 4, 1, 3, 5).reshape(-1, side_count * side_count, channels)

def from_grid(grouped, samples, row_count, col_count, side_count):
    channels = grouped.shape[-1]
    unfolded = grouped.reshape(samples, row_count // side_count, col_count // side_count, side_count, side_count, channels)
    return unfolded.transpose(0, 3, 1, 4, 2, 5).reshape(samples, row_count, col_count, channels)

def attend(queries, key_rows, value_rows, bias_full, head_size):
    groups, members, channels = queries.shape
    head_count = channels // head_size
    query_heads = queries.astype(jnp.float32).reshape(groups, members, head_count, head_size)
    key_heads = key_rows.astype(jnp.float32).reshape(groups, members, head_count, head_size)
    value_heads = value_rows.astype(jnp.float32).reshape(groups, members, head_count, head_size)
    scores = jnp.einsum('gqhd,gkhd->ghqk', query_heads, key_heads, precision=lax.Precision.HIGHEST)
    scores = scores * head_size ** (-0.5) + bias_full[None]
    highest = lax.optimization_barrier(jnp.max(scores, axis=-1, keepdims=True))
    lifted = jnp.exp(scores - highest)
    weights = lax.optimization_barrier((lifted / lax.optimization_barrier(jnp.sum(lifted, axis=-1, keepdims=True))).astype(jnp.bfloat16))
    blended = jnp.einsum('ghqk,gkhd->gqhd', weights.astype(jnp.float32), value_heads, precision=lax.Precision.HIGHEST)
    return blended.astype(jnp.bfloat16).reshape(groups, members, channels)

def grouped_attention(grouped, weight, bias_full, head_size):
    groups, members, channels = grouped.shape
    projected = jnp.dot(grouped.reshape(groups * members, channels), weight, preferred_element_type=jnp.float32)
    projected = lax.optimization_barrier(projected.astype(jnp.bfloat16)).reshape(groups, members, 3 * channels)
    return attend(projected[..., :channels], projected[..., channels:2 * channels], projected[..., 2 * channels:], bias_full, head_size)

def blocked_attention(grouped, weight, bias_full, head_size):
    group_count, members, channels = grouped.shape
    blocks = grouped.reshape(group_count // 64, 64, members, channels)
    result = lax.map(lambda block_rows: grouped_attention(block_rows, weight, bias_full, head_size), blocks)
    return result.reshape(group_count, members, channels)

def reference(latent, context, conv_weight, window_qkv, window_out, window_bias, grid_qkv, grid_out, grid_bias, mlp_gain, mlp_in, mlp_out):
    window_table = bias_lookup(window_bias)
    grid_table = bias_lookup(grid_bias)

    def one_sample(inputs):
        fine_grid, coarse = inputs
        row_count, col_count, channels = fine_grid.shape
        computed = lax.conv_general_dilated(coarse[None].astype(jnp.float32), conv_weight.astype(jnp.float32), (1, 1), ((1, 1), (1, 1)), dimension_numbers=('NHWC', 'HWIO', 'NHWC'), precision=lax.Precision.HIGHEST)
        features = lax.optimization_barrier(computed.astype(jnp.bfloat16))
        padded = jnp.pad(features, ((0, 0), (1, 1), (1, 1), (0, 0))).astype(jnp.float32)
        lifted_rows = upsample(padded, 1)
        lifted_rows = jnp.pad(lifted_rows, ((0, 0), (0, 0), (0, 0), (0, 0)))
        upsampled = upsample(lifted_rows, 2)
        residual_a = fine_grid[None] + upsampled
        normed = layer_norm(residual_a).astype(jnp.bfloat16)
        window_heads = from_windows(blocked_attention(to_windows(normed, WIN), window_qkv, window_table, HEAD), 1, row_count, col_count, WIN)
        residual_b = residual_a + project(window_heads, window_out)
        normed = layer_norm(residual_b).astype(jnp.bfloat16)
        grid_heads = from_grid(blocked_attention(to_grid(normed, WIN), grid_qkv, grid_table, HEAD), 1, row_count, col_count, WIN)
        residual_c = residual_b + project(grid_heads, grid_out)
        normed = (layer_norm(residual_c) * mlp_gain).astype(jnp.bfloat16)
        hidden = jax.nn.gelu(project(normed, mlp_in)).astype(jnp.bfloat16)
        return (residual_c + project(hidden, mlp_out))[0]
    return lax.map(one_sample, (latent, context))
```

```python
import functools

import jax
import jax.numpy as jnp
import numpy as np
from jax import lax
from jax.experimental import pallas as pl
from jax.experimental.pallas import tpu as pltpu
from jax.sharding import PartitionSpec as P

HEAD = 32
WIN = 8
NORM_EPS = 1e-05
LANES = 128
JOINT = ("wide", "narrow")


def neighbours(block, axis, dim, width):
    count = lax.axis_size(axis)
    forward = [(i, i + 1) for i in range(count - 1)]
    backward = [(target, source) for source, target in forward]
    low = lax.ppermute(
        lax.slice_in_dim(block, block.shape[dim] - width, None, axis=dim), axis, forward
    )
    high = lax.ppermute(lax.slice_in_dim(block, 0, width, axis=dim), axis, backward)
    return low, high


def shifted_bias(tables):
    side = WIN
    rows = jnp.stack([tables[:, :, side - 1 - c : 2 * side - 1 - c] for c in range(side)], axis=1)
    flat = rows.reshape(tables.shape[0], side, (2 * side - 1) * side)
    return jnp.pad(flat, ((0, 0), (0, 0), (0, LANES - flat.shape[2])))


def fill_bias(shifted_ref, table_ref):
    heads = shifted_ref.shape[0]
    low_half = lax.broadcasted_iota(jnp.int32, (WIN, LANES), 1) < WIN * WIN
    for pair in range(heads // 2):
        even = shifted_ref[2 * pair]
        odd = shifted_ref[2 * pair + 1]
        for key_row in range(WIN):
            start = WIN * (WIN - 1 - key_row)
            even_part = pltpu.roll(even, (LANES - start) % LANES, 1)
            odd_part = pltpu.roll(odd, (LANES - start + WIN * WIN) % LANES, 1)
            table_ref[key_row * WIN : (key_row + 1) * WIN, pair * LANES : (pair + 1) * LANES] = (
                jnp.where(low_half, even_part, odd_part)
            )


def layer_norm(values):
    center = values - jnp.mean(values, axis=-1, keepdims=True)
    spread = jnp.mean(center * center, axis=-1, keepdims=True)
    return center * lax.rsqrt(spread + NORM_EPS)


def attend(qk_ref, vt_ref, bias_ref, row_start, lane_start, half, channels):
    members = WIN * WIN
    lane_head = lax.broadcasted_iota(jnp.int32, (members, LANES), 1) // HEAD
    low_half = lax.broadcasted_iota(jnp.int32, (HEAD, LANES), 1) < members
    per = LANES // HEAD
    pieces = []
    for block in range(channels // LANES):
        queries = qk_ref[pl.ds(row_start, members), block * LANES : (block + 1) * LANES]
        keys = qk_ref[
            pl.ds(row_start, members),
            channels + block * LANES : channels + (block + 1) * LANES,
        ]
        zero = jnp.zeros_like(queries)
        spread = jnp.concatenate(
            [jnp.where(lane_head == h, queries, zero) for h in range(per)], axis=0
        )
        scores = lax.dot_general(
            keys, spread, (((1,), (1,)), ((), ())), preferred_element_type=jnp.float32
        )
        wide = per * members
        scores = scores * HEAD ** (-0.5) + bias_ref[:, block * wide : (block + 1) * wide]
        lifted = jnp.exp(scores - jnp.max(scores, axis=0, keepdims=True))
        weights = lifted * (1.0 / jnp.sum(lifted, axis=0, keepdims=True))
        weights = weights.astype(jnp.bfloat16)
        for pair in range(per // 2):
            first = block * LANES + pair * 2 * HEAD
            values = vt_ref[first : first + 2 * HEAD, pl.ds(lane_start, LANES)]
            values = values[:, half * members : (half + 1) * members]
            mixed = jnp.dot(
                values,
                weights[:, pair * LANES : (pair + 1) * LANES],
                preferred_element_type=jnp.float32,
            )
            pieces.append(jnp.where(low_half, mixed[:HEAD], mixed[HEAD:]))
    turned = jnp.concatenate(pieces, axis=0).T
    return jnp.concatenate([turned[:members], turned[members:]], axis=1)


def out_copies(weight_ref, buffer_ref, sem):
    pairs = weight_ref.shape[0] // (2 * HEAD)
    return [
        pltpu.make_async_copy(
            weight_ref.at[pl.ds((2 * pair + parity) * HEAD, HEAD)],
            buffer_ref.at[pl.ds((parity * pairs + pair) * HEAD, HEAD)],
            sem,
        )
        for parity in range(2)
        for pair in range(pairs)
    ]


def window_kernel(
    place_ref,
    latent_ref,
    context_ref,
    low_ref,
    high_ref,
    left_ref,
    right_ref,
    lift_ref,
    shifted_ref,
    conv_hbm,
    qkv_hbm,
    vt_hbm,
    out_hbm,
    residual_ref,
    normed_ref,
    conv_w,
    qk_w,
    vt_w,
    out_w,
    wide_s,
    taps_s,
    features_s,
    normed_s,
    qk_s,
    vt_s,
    heads_s,
    bias_s,
    sems,
    *,
    stride,
):
    rows, cols, channels = latent_ref.shape
    half_rows, half_cols, coarse = context_ref.shape
    members = WIN * WIN
    windows = cols // WIN
    copies = [
        pltpu.make_async_copy(conv_hbm, conv_w, sems.at[0]),
        pltpu.make_async_copy(qkv_hbm.at[:, pl.ds(0, 2 * channels)], qk_w, sems.at[1]),
        pltpu.make_async_copy(vt_hbm, vt_w, sems.at[2]),
    ]
    placed = out_copies(out_hbm, out_w, sems.at[3])
    for copy in copies + placed:
        copy.start()
    span = half_rows + 2
    wide_s[...] = jnp.zeros_like(wide_s)
    for row in range(half_rows + 4):
        base = row * stride
        if row < 2:
            middle = low_ref[row]
        elif row < half_rows + 2:
            middle = context_ref[row - 2]
        else:
            middle = high_ref[row - half_rows - 2]
        wide_s[base : base + 2] = left_ref[row].astype(jnp.float32)
        wide_s[base + 2 : base + 2 + half_cols] = middle.astype(jnp.float32)
        wide_s[base + 2 + half_cols : base + 4 + half_cols] = right_ref[row].astype(jnp.float32)
    tall = (half_rows + 4) * stride
    for shift in range(3):
        taps_s[:, shift * coarse : (shift + 1) * coarse] = wide_s[shift : shift + tall].astype(
            jnp.bfloat16
        )
    fill_bias(shifted_ref, bias_s)
    copies[0].wait()
    total = jnp.zeros((span * stride, channels), jnp.float32)
    for shift in range(3):
        total = total + jnp.dot(
            taps_s[shift * stride : (shift + span) * stride],
            conv_w[shift],
            preferred_element_type=jnp.float32,
        )
    flat = lax.broadcasted_iota(jnp.int32, (span * stride, 1), 0)
    row_place = flat // stride + place_ref[0]
    col_place = flat % stride + place_ref[1]
    inside = (row_place >= 0) & (row_place < place_ref[2])
    inside = inside & (col_place >= 0) & (col_place < place_ref[3])
    inside = inside & (flat % stride < half_cols + 2)
    features_s[...] = jnp.where(inside, total, 0.0).astype(jnp.bfloat16)

    for window in range(windows):
        cells = latent_ref[:, window * WIN : (window + 1) * WIN, :].reshape(members, channels)
        lifted = jnp.dot(lift_ref[window], features_s[...], preferred_element_type=jnp.float32)
        residual = cells + lifted
        residual_ref[window] = residual
        normed_s[window * members : (window + 1) * members] = layer_norm(residual).astype(
            jnp.bfloat16
        )

    copies[1].wait()
    for block in range(4):
        part = slice(block * channels // 2, (block + 1) * channels // 2)
        qk_s[:, part] = jnp.dot(
            normed_s[...], qk_w[:, part], preferred_element_type=jnp.float32
        ).astype(jnp.bfloat16)
    copies[2].wait()
    vt_s[...] = lax.dot_general(
        vt_w[...], normed_s[...], (((1,), (1,)), ((), ())), preferred_element_type=jnp.float32
    ).astype(jnp.bfloat16)

    def two_windows(step, carry):
        for half in range(2):
            row_start = pl.multiple_of((2 * step + half) * members, members)
            heads = attend(
                qk_s, vt_s, bias_s, row_start, pl.multiple_of(step * LANES, LANES), half, channels
            )
            heads_s[pl.ds(row_start, members)] = heads.astype(jnp.bfloat16)
        return carry

    lax.fori_loop(0, windows // 2, two_windows, 0)
    for copy in placed:
        copy.wait()
    narrow = normed_ref.shape[1]
    for window in range(windows):
        part = slice(window * members, (window + 1) * members)
        residual = residual_ref[window] + jnp.dot(
            heads_s[part], out_w[...], preferred_element_type=jnp.float32
        )
        residual_ref[window] = residual
        normed = layer_norm(residual).astype(jnp.bfloat16).reshape(rows, WIN, channels)
        normed_ref[:, window % narrow, window // narrow] = normed


def grid_kernel(
    cells_ref,
    shifted_ref,
    qkv_hbm,
    vt_hbm,
    heads_ref,
    qk_w,
    vt_w,
    spread_s,
    normed_s,
    qk_s,
    vt_s,
    bias_s,
    sems,
):
    members, groups, channels = cells_ref.shape
    copies = [
        pltpu.make_async_copy(qkv_hbm.at[:, pl.ds(0, 2 * channels)], qk_w, sems.at[0]),
        pltpu.make_async_copy(vt_hbm, vt_w, sems.at[1]),
    ]
    for copy in copies:
        copy.start()
    fill_bias(shifted_ref, bias_s)
    spread_s[...] = cells_ref[...].astype(jnp.float32)
    for group in range(groups):
        normed_s[group * members : (group + 1) * members] = spread_s[:, group, :].astype(
            jnp.bfloat16
        )
    copies[0].wait()
    for block in range(4):
        part = slice(block * channels // 2, (block + 1) * channels // 2)
        qk_s[:, part] = jnp.dot(
            normed_s[...], qk_w[:, part], preferred_element_type=jnp.float32
        ).astype(jnp.bfloat16)
    copies[1].wait()
    vt_s[...] = lax.dot_general(
        vt_w[...], normed_s[...], (((1,), (1,)), ((), ())), preferred_element_type=jnp.float32
    ).astype(jnp.bfloat16)

    for step in range(groups // 2):
        for half in range(2):
            group = 2 * step + half
            heads = attend(
                qk_s, vt_s, bias_s, group * members, step * LANES, half, channels
            )
            spread_s[:, group, :] = heads
    heads_ref[...] = spread_s[...].astype(jnp.bfloat16)


def mlp_kernel(
    residual_ref,
    heads_ref,
    gain_ref,
    out_hbm,
    first_hbm,
    second_hbm,
    result_ref,
    out_w,
    first_w,
    second_w,
    residual_s,
    normed_s,
    sems,
):
    windows, members, channels = residual_ref.shape
    rows, narrow = heads_ref.shape[:2]
    hidden = first_w.shape[1]
    placed = out_copies(out_hbm, out_w, sems.at[0])
    copies = [
        pltpu.make_async_copy(first_hbm, first_w, sems.at[1]),
        pltpu.make_async_copy(second_hbm, second_w, sems.at[2]),
    ]
    for copy in placed + copies:
        copy.start()
    for copy in placed:
        copy.wait()
    for window in range(windows):
        heads = heads_ref[:, window % narrow, window // narrow].reshape(members, channels)
        residual = residual_ref[window] + jnp.dot(
            heads, out_w[...], preferred_element_type=jnp.float32
        )
        part = slice(window * members, (window + 1) * members)
        residual_s[part] = residual
        normed_s[part] = (layer_norm(residual) * gain_ref[...]).astype(jnp.bfloat16)
    for copy in copies:
        copy.wait()
    step_size = channels // 2

    def one_block(step, carry):
        start = pl.multiple_of(step * step_size, step_size)
        inner = jnp.dot(
            normed_s[...], first_w[:, pl.ds(start, step_size)], preferred_element_type=jnp.float32
        )
        cubed = 0.7978845608028654 * (inner + 0.044715 * (inner * inner * inner))
        active = (0.5 * inner * (1.0 + jnp.tanh(cubed))).astype(jnp.bfloat16)
        residual_s[...] += jnp.dot(
            active, second_w[pl.ds(start, step_size)], preferred_element_type=jnp.float32
        )
        return carry

    lax.fori_loop(0, hidden // step_size, one_block, 0)
    for window in range(windows):
        result_ref[:, window * WIN : (window + 1) * WIN, :] = residual_s[
            window * members : (window + 1) * members
        ].reshape(rows, WIN, channels)


VMEM = pl.BlockSpec(memory_space=pltpu.MemorySpace.VMEM)
ANY = pl.BlockSpec(memory_space=pl.ANY)
SMEM = pl.BlockSpec(memory_space=pltpu.MemorySpace.SMEM)
PARAMS = dict(vmem_limit_bytes=48 * 1024 * 1024)


def lift_matrix(rows, cols, stride):
    def along(count):
        fine = np.arange(count)
        place = np.zeros((count, count // 2 + 2), np.float32)
        middle = fine // 2 + 1
        place[fine, middle] = 0.75
        place[fine, middle + np.where(fine % 2 == 0, -1, 1)] = 0.25
        return place

    by_row = along(rows)
    by_col = along(cols)
    by_col = np.pad(by_col, ((0, 0), (0, stride - by_col.shape[1])))
    both = by_row[:, None, :, None] * by_col[None, :, None, :]
    both = both.reshape(rows, cols // WIN, WIN, -1).transpose(1, 0, 2, 3)
    return jnp.asarray(both.reshape(cols // WIN, rows * WIN, -1), jnp.bfloat16)


def on_device(
    latent,
    context,
    conv_weight,
    window_qkv,
    window_out,
    window_bias,
    grid_qkv,
    grid_out,
    grid_bias,
    mlp_gain,
    mlp_in,
    mlp_out,
):
    samples, rows, cols, channels = latent.shape
    wide_count = lax.axis_size("wide")
    narrow = lax.axis_size("narrow")
    half_rows, half_cols, coarse = context.shape[1:]
    hidden = mlp_in.shape[1]
    members = WIN * WIN
    windows = cols // WIN
    planes = WIN // narrow
    split = wide_count // WIN
    assert rows == WIN and planes * narrow == WIN and split * WIN == wide_count
    assert windows == planes * narrow and WIN % split == 0
    stride = -(-(half_cols + 4) // 16) * 16

    low, high = neighbours(context, "wide", 1, 2)
    widened = jnp.concatenate([low, context, high], axis=1)
    left, right = neighbours(widened, "narrow", 2, 2)
    shifted = shifted_bias(jnp.concatenate([window_bias, grid_bias], axis=0))
    heads_count = window_bias.shape[0]
    window_shifted, grid_shifted = shifted[:heads_count], shifted[heads_count:]
    window_vt = window_qkv[:, 2 * channels :].T
    grid_vt = grid_qkv[:, 2 * channels :].T
    lift = lift_matrix(rows, cols, stride)
    conv_flat = conv_weight.reshape(3, 3 * coarse, channels)
    place = jnp.stack(
        [
            lax.axis_index("wide") * half_rows - 1,
            lax.axis_index("narrow") * half_cols - 1,
            jnp.int32(wide_count * half_rows),
            jnp.int32(narrow * half_cols),
        ]
    ).astype(jnp.int32)

    bf16, f32 = jnp.bfloat16, jnp.float32
    tokens = rows * cols
    span = half_rows + 2
    window_call = pl.pallas_call(
        functools.partial(window_kernel, stride=stride),
        out_shape=(
            jax.ShapeDtypeStruct((windows, members, channels), f32),
            jax.ShapeDtypeStruct((rows, narrow, planes, WIN, channels), bf16),
        ),
        in_specs=[SMEM] + [VMEM] * 8 + [ANY] * 4,
        out_specs=(VMEM, VMEM),
        scratch_shapes=[
            pltpu.VMEM((3, 3 * coarse, channels), bf16),
            pltpu.VMEM((channels, 2 * channels), bf16),
            pltpu.VMEM((channels, channels), bf16),
            pltpu.VMEM((channels, channels), bf16),
            pltpu.VMEM(((half_rows + 4) * stride + 16, coarse), f32),
            pltpu.VMEM(((half_rows + 4) * stride, 3 * coarse), bf16),
            pltpu.VMEM((span * stride, channels), bf16),
            pltpu.VMEM((tokens, channels), bf16),
            pltpu.VMEM((tokens, 2 * channels), bf16),
            pltpu.VMEM((channels, tokens), bf16),
            pltpu.VMEM((tokens, channels), bf16),
            pltpu.VMEM((members, heads_count * members), f32),
            pltpu.SemaphoreType.DMA((4,)),
        ],
        compiler_params=pltpu.CompilerParams(**PARAMS),
        name="window",
    )
    groups = WIN
    grid_call = pl.pallas_call(
        grid_kernel,
        out_shape=jax.ShapeDtypeStruct((members, groups, channels), bf16),
        in_specs=[VMEM] * 2 + [ANY] * 2,
        out_specs=VMEM,
        scratch_shapes=[
            pltpu.VMEM((channels, 2 * channels), bf16),
            pltpu.VMEM((channels, channels), bf16),
            pltpu.VMEM((members, groups, channels), f32),
            pltpu.VMEM((tokens, channels), bf16),
            pltpu.VMEM((tokens, 2 * channels), bf16),
            pltpu.VMEM((channels, tokens), bf16),
            pltpu.VMEM((members, heads_count * members), f32),
            pltpu.SemaphoreType.DMA((2,)),
        ],
        compiler_params=pltpu.CompilerParams(**PARAMS),
        name="grid",
    )
    mlp_call = pl.pallas_call(
        mlp_kernel,
        out_shape=jax.ShapeDtypeStruct((rows, cols, channels), f32),
        in_specs=[VMEM] * 3 + [ANY] * 3,
        out_specs=VMEM,
        scratch_shapes=[
            pltpu.VMEM((channels, channels), bf16),
            pltpu.VMEM((channels, hidden), bf16),
            pltpu.VMEM((hidden, channels), bf16),
            pltpu.VMEM((tokens, channels), f32),
            pltpu.VMEM((tokens, channels), bf16),
            pltpu.SemaphoreType.DMA((3,)),
        ],
        compiler_params=pltpu.CompilerParams(**PARAMS),
        name="mlp",
    )
    gain = mlp_gain.reshape(1, channels)

    def send(normed):
        pieces = normed.reshape(rows, narrow, planes, split, WIN // split, channels)
        pieces = pieces.transpose(0, 3, 1, 2, 4, 5)
        pieces = pieces.reshape(wide_count * narrow, planes, WIN // split, channels)
        received = lax.all_to_all(pieces, JOINT, split_axis=0, concat_axis=0, tiled=True)
        received = received.reshape(WIN, split, narrow, planes, WIN // split, channels)
        return received.transpose(0, 2, 3, 1, 4, 5).reshape(members, WIN, channels)

    def send_back(heads):
        pieces = heads.reshape(WIN, narrow, planes, split, WIN // split, channels)
        pieces = pieces.transpose(0, 3, 1, 2, 4, 5)
        pieces = pieces.reshape(wide_count * narrow, planes, WIN // split, channels)
        received = lax.all_to_all(pieces, JOINT, split_axis=0, concat_axis=0, tiled=True)
        received = received.reshape(rows, split, narrow, planes, WIN // split, channels)
        return received.transpose(0, 2, 3, 1, 4, 5).reshape(rows, narrow, planes, WIN, channels)

    residuals, cells = [], []
    for sample in range(samples):
        residual, normed = window_call(
            place,
            latent[sample],
            context[sample],
            low[sample],
            high[sample],
            left[sample],
            right[sample],
            lift,
            window_shifted,
            conv_flat,
            window_qkv,
            window_vt,
            window_out,
        )
        residuals.append(residual)
        cells.append(send(normed))
    returned = []
    for sample in range(samples):
        heads = grid_call(cells[sample], grid_shifted, grid_qkv, grid_vt)
        returned.append(send_back(heads))
    results = [
        mlp_call(residuals[sample], returned[sample], gain, grid_out, mlp_in, mlp_out)
        for sample in range(samples)
    ]
    return jnp.stack(results)


def solution(mesh):
    return jax.shard_map(
        on_device,
        mesh=mesh,
        in_specs=(
            P(None, "wide", "narrow", None),
            P(None, "wide", "narrow", None),
        )
        + (P(),) * 10,
        out_specs=P(None, "wide", "narrow", None),
        check_vma=False,
    )
```

```python
import functools
import math

import jax
import jax.numpy as jnp
import numpy as np
from jax import lax
from jax.experimental import pallas as pl
from jax.experimental.pallas import tpu as pltpu
from jax.sharding import PartitionSpec as P

HEAD = 32
WIN = 8
NORM_EPS = 1e-05
LANES = 128
LOG2E = math.log2(math.e)
JOINT = ("wide", "narrow")


def neighbours(block, axis, dim, width):
    count = lax.axis_size(axis)
    forward = [(i, i + 1) for i in range(count - 1)]
    backward = [(target, source) for source, target in forward]
    low = lax.ppermute(
        lax.slice_in_dim(block, block.shape[dim] - width, None, axis=dim), axis, forward
    )
    high = lax.ppermute(lax.slice_in_dim(block, 0, width, axis=dim), axis, backward)
    return low, high


def bias_kernel(flat_ref, pick_ref, window_ref, grid_ref, spread_s):
    both, places = flat_ref.shape
    side = WIN
    flat = flat_ref[...] * LOG2E
    top = flat.astype(jnp.bfloat16)
    rest = flat - top.astype(jnp.float32)
    middle = rest.astype(jnp.bfloat16)
    last = (rest - middle.astype(jnp.float32)).astype(jnp.bfloat16)
    stacked = jnp.concatenate([top, middle, last], axis=0)
    for key_col in range(side):
        picked = jnp.dot(stacked, pick_ref[key_col], preferred_element_type=jnp.float32)
        spread_s[pl.ds(key_col, both, stride=side), :] = (
            picked[:both] + picked[both : 2 * both]
        ) + picked[2 * both :]
    low_half = lax.broadcasted_iota(jnp.int32, (side, LANES), 1) < side * side
    heads = both // 2
    for table, table_ref in enumerate((window_ref, grid_ref)):
        for pair in range(heads // 2):
            base = (table * heads + 2 * pair) * side
            even = spread_s[base : base + side]
            odd = spread_s[base + side : base + 2 * side]
            for key_row in range(side):
                start = side * (side - 1 - key_row)
                even_part = pltpu.roll(even, (LANES - start) % LANES, 1)
                odd_part = pltpu.roll(odd, (LANES - start + side * side) % LANES, 1)
                table_ref[
                    key_row * side : (key_row + 1) * side, pair * LANES : (pair + 1) * LANES
                ] = jnp.where(low_half, even_part, odd_part)


def bias_pick(places):
    side = WIN
    span = 2 * side - 1
    pick = np.zeros((side, places, LANES), np.float32)
    for c in range(side):
        for a in range(span):
            for j in range(side):
                pick[c, a * span + j + side - 1 - c, a * side + j] = 1.0
    return jnp.asarray(pick, jnp.bfloat16)


def layer_norm(values):
    center = values - jnp.mean(values, axis=-1, keepdims=True)
    spread = jnp.mean(center * center, axis=-1, keepdims=True)
    return center * lax.rsqrt(spread + NORM_EPS)


def project(normed_s, qk_w, vt_w, qk_s, vt_s, waits):
    channels = normed_s.shape[1]
    waits[0].wait()
    queries = jnp.dot(
        normed_s[...], qk_w[:, :channels], preferred_element_type=jnp.float32
    )
    qk_s[:, :channels] = (queries * (LOG2E * HEAD ** (-0.5))).astype(jnp.bfloat16)
    qk_s[:, channels:] = jnp.dot(
        normed_s[...], qk_w[:, channels:], preferred_element_type=jnp.float32
    ).astype(jnp.bfloat16)
    waits[1].wait()
    values = lax.dot_general(
        vt_w[...], normed_s[...], (((1,), (1,)), ((), ())), preferred_element_type=jnp.float32
    ).astype(jnp.bfloat16)
    pairs, tall = vt_s.shape[:2]
    for pair in range(pairs):
        vt_s[pair, : 2 * HEAD] = values[pair * 2 * HEAD : (pair + 1) * 2 * HEAD]
        vt_s[pair, 2 * HEAD :] = jnp.ones((tall - 2 * HEAD, values.shape[1]), jnp.bfloat16)


def attend(groups, qk_s, vt_s, bias_s, score_s, top_s, lifted_s, store):
    members = WIN * WIN
    channels = qk_s.shape[1] // 2
    blocks = channels // LANES
    per = LANES // HEAD
    wide = per * members
    lane_head = lax.broadcasted_iota(jnp.int32, (members, LANES), 1) // HEAD
    own = [lane_head == h for h in range(per)]
    low_half = lax.broadcasted_iota(jnp.int32, (HEAD, LANES), 1) < members

    def scores(group, block):
        rows = slice(group * members, (group + 1) * members)
        part = slice(block * wide, (block + 1) * wide)
        queries = qk_s[rows, block * LANES : (block + 1) * LANES]
        keys = qk_s[rows, channels + block * LANES : channels + (block + 1) * LANES]
        zero = jnp.zeros_like(queries)
        spread = jnp.concatenate([jnp.where(mask, queries, zero) for mask in own], axis=0)
        score = lax.dot_general(
            keys, spread, (((1,), (1,)), ((), ())), preferred_element_type=jnp.float32
        )
        score = score + bias_s[:, part]
        score_s[group % 2, :, part] = score
        top_s[group % 2, :, part] = jnp.max(score, axis=0, keepdims=True)

    def lift(group, block):
        part = slice(block * wide, (block + 1) * wide)
        lifted = jnp.exp2(score_s[group % 2, :, part] - top_s[group % 2, :, part])
        lifted_s[group % 2, :, part] = lifted.astype(jnp.bfloat16)

    def blend(group, block):
        pieces = []
        for pair in range(block * per // 2, (block + 1) * per // 2):
            values = vt_s[pair, :, group * members : (group + 1) * members]
            mixed = jnp.dot(
                values,
                lifted_s[group % 2, :, pair * LANES : (pair + 1) * LANES],
                preferred_element_type=jnp.float32,
            )
            chosen = jnp.where(low_half, mixed[:HEAD], mixed[HEAD : 2 * HEAD])
            pieces.append(chosen * (1.0 / mixed[2 * HEAD : 2 * HEAD + 1]))
        return pieces

    for step in range(groups + 2):
        pieces = []
        for block in range(blocks):
            if step < groups:
                scores(step, block)
            if 0 <= step - 1 < groups:
                lift(step - 1, block)
            if step >= 2:
                pieces.extend(blend(step - 2, block))
        if pieces:
            turned = jnp.concatenate(pieces, axis=0).T
            store(step - 2, jnp.concatenate([turned[:members], turned[members:]], axis=1))


def out_copies(weight_ref, buffer_ref, sem):
    pairs = weight_ref.shape[0] // (2 * HEAD)
    return [
        pltpu.make_async_copy(
            weight_ref.at[pl.ds((2 * pair + parity) * HEAD, HEAD)],
            buffer_ref.at[pl.ds((parity * pairs + pair) * HEAD, HEAD)],
            sem,
        )
        for parity in range(2)
        for pair in range(pairs)
    ]


def window_kernel(
    place_ref,
    latent_hbm,
    context_hbm,
    low_hbm,
    high_hbm,
    left_hbm,
    right_hbm,
    lift_hbm,
    bias_hbm,
    conv_hbm,
    qkv_hbm,
    vt_hbm,
    out_hbm,
    residual_hbm,
    normed_hbm,
    latent_ref,
    context_ref,
    low_ref,
    high_ref,
    left_ref,
    right_ref,
    lift_ref,
    bias_s,
    conv_w,
    qk_w,
    vt_w,
    out_w,
    wide_s,
    taps_s,
    features_s,
    residual_ref,
    normed_s,
    qk_s,
    vt_s,
    score_s,
    top_s,
    lifted_s,
    heads_s,
    sent_s,
    sems,
    out_sems,
    *,
    stride,
    sample,
):
    rows, cols, channels = latent_ref.shape
    half_rows, half_cols, coarse = context_ref.shape
    members = WIN * WIN
    windows = cols // WIN
    halo = [
        pltpu.make_async_copy(source.at[sample], target, sems.at[0])
        for source, target in (
            (context_hbm, context_ref),
            (low_hbm, low_ref),
            (high_hbm, high_ref),
            (left_hbm, left_ref),
            (right_hbm, right_ref),
        )
    ]
    conv_copy = pltpu.make_async_copy(conv_hbm, conv_w, sems.at[1])
    cells_copies = [
        pltpu.make_async_copy(lift_hbm, lift_ref, sems.at[2]),
        pltpu.make_async_copy(latent_hbm.at[sample], latent_ref, sems.at[2]),
    ]
    qk_copy = pltpu.make_async_copy(qkv_hbm.at[:, pl.ds(0, 2 * channels)], qk_w, sems.at[3])
    vt_copy = pltpu.make_async_copy(vt_hbm, vt_w, sems.at[4])
    bias_copy = pltpu.make_async_copy(bias_hbm, bias_s, sems.at[5])
    placed = out_copies(out_hbm, out_w, sems.at[6])
    for copy in halo + [conv_copy] + cells_copies + [qk_copy, vt_copy, bias_copy] + placed:
        copy.start()
    span = half_rows + 2
    for copy in halo:
        copy.wait()
    for row in range(half_rows + 4):
        base = row * stride
        if row < 2:
            middle = low_ref[row]
        elif row < half_rows + 2:
            middle = context_ref[row - 2]
        else:
            middle = high_ref[row - half_rows - 2]
        wide_s[base + 6 : base + 8] = left_ref[row].astype(jnp.float32)
        wide_s[base + 8 : base + 8 + half_cols] = middle.astype(jnp.float32)
        wide_s[base + 8 + half_cols : base + 10 + half_cols] = right_ref[row].astype(jnp.float32)
    tall = (half_rows + 4) * stride
    for shift in range(3):
        taps_s[:, shift * coarse : (shift + 1) * coarse] = wide_s[
            shift + 6 : shift + 6 + tall
        ].astype(jnp.bfloat16)
    conv_copy.wait()
    patches = jnp.concatenate(
        [taps_s[shift * stride : (shift + span) * stride] for shift in range(3)], axis=1
    )
    total = jnp.dot(patches, conv_w[...], preferred_element_type=jnp.float32)
    column = lax.broadcasted_iota(jnp.int32, (stride, channels), 0)
    col_place = column + place_ref[1]
    col_inside = (col_place >= 0) & (col_place < place_ref[3]) & (column < half_cols + 2)
    for row in range(span):
        row_place = place_ref[0] + row
        inside = col_inside & ((row_place >= 0) & (row_place < place_ref[2]))
        part = slice(row * stride, (row + 1) * stride)
        features_s[part] = jnp.where(inside, total[part], 0.0).astype(jnp.bfloat16)

    for copy in cells_copies:
        copy.wait()
    residual_ref[...] = jnp.dot(
        lift_ref[...], features_s[...], preferred_element_type=jnp.float32
    )
    for window in range(windows):
        part = slice(window * members, (window + 1) * members)
        cells = latent_ref[:, window * WIN : (window + 1) * WIN, :].reshape(members, channels)
        residual = cells + residual_ref[part]
        residual_ref[part] = residual
        normed_s[part] = layer_norm(residual).astype(jnp.bfloat16)

    project(normed_s, qk_w, vt_w, qk_s, vt_s, (qk_copy, vt_copy))
    bias_copy.wait()

    def store_heads(window, heads):
        heads_s[window * members : (window + 1) * members] = heads.astype(jnp.bfloat16)

    attend(windows, qk_s, vt_s, bias_s, score_s, top_s, lifted_s, store_heads)
    for copy in placed:
        copy.wait()
    residual_ref[...] += jnp.dot(heads_s[...], out_w[...], preferred_element_type=jnp.float32)
    narrow = normed_hbm.shape[1]
    for window in range(windows):
        part = slice(window * members, (window + 1) * members)
        normed = layer_norm(residual_ref[part]).astype(jnp.bfloat16)
        sent_s[:, window % narrow, window // narrow] = normed.reshape(rows, WIN, channels)
    stores = [
        pltpu.make_async_copy(sent_s, normed_hbm, out_sems.at[0]),
        pltpu.make_async_copy(residual_ref, residual_hbm, out_sems.at[1]),
    ]
    for store in stores:
        store.start()
    for store in stores:
        store.wait()


def grid_kernel(
    cells_hbm,
    bias_hbm,
    qkv_hbm,
    vt_hbm,
    heads_hbm,
    cells_ref,
    qk_w,
    vt_w,
    spread_s,
    normed_s,
    qk_s,
    vt_s,
    score_s,
    top_s,
    lifted_s,
    bias_s,
    sems,
):
    tokens, channels = cells_ref.shape
    groups = WIN
    members = tokens // groups
    copies = [
        pltpu.make_async_copy(cells_hbm, cells_ref, sems.at[0]),
        pltpu.make_async_copy(qkv_hbm.at[:, pl.ds(0, 2 * channels)], qk_w, sems.at[1]),
        pltpu.make_async_copy(vt_hbm, vt_w, sems.at[2]),
        pltpu.make_async_copy(bias_hbm, bias_s, sems.at[3]),
    ]
    for copy in copies:
        copy.start()
    copies[0].wait()
    lanes = [slice(start, start + LANES) for start in range(0, channels, LANES)]
    for chunk, lane in enumerate(lanes):
        spread_s[chunk] = cells_ref[:, lane].astype(jnp.float32)
    for group in range(groups):
        for chunk, lane in enumerate(lanes):
            normed_s[group * members : (group + 1) * members, lane] = spread_s[
                chunk, pl.ds(group, members, stride=groups), :
            ].astype(jnp.bfloat16)
    project(normed_s, qk_w, vt_w, qk_s, vt_s, copies[1:3])
    copies[3].wait()

    def store_heads(group, heads):
        for chunk, lane in enumerate(lanes):
            spread_s[chunk, pl.ds(group, members, stride=groups), :] = heads[:, lane]

    attend(groups, qk_s, vt_s, bias_s, score_s, top_s, lifted_s, store_heads)
    for chunk, lane in enumerate(lanes):
        cells_ref[:, lane] = spread_s[chunk].astype(jnp.bfloat16)
    store = pltpu.make_async_copy(cells_ref, heads_hbm, sems.at[0])
    store.start()
    store.wait()


def mlp_kernel(
    *refs,
    sample,
):
    (
        residual_hbm,
        heads_hbm,
        gain_ref,
        out_hbm,
        first_hbm,
        second_hbm,
    ) = refs[:6]
    (
        result_hbm,
        residual_ref,
        heads_ref,
        out_w,
        first_w,
        second_w,
        residual_s,
        normed_s,
        active_s,
        sems,
    ) = refs[-10:]
    tokens, channels = residual_ref.shape
    members = WIN * WIN
    windows = tokens // members
    rows, narrow = heads_ref.shape[:2]
    hidden = first_w.shape[1]
    placed = out_copies(out_hbm, out_w, sems.at[0])
    cells = [
        pltpu.make_async_copy(heads_hbm, heads_ref, sems.at[3]),
        pltpu.make_async_copy(residual_hbm, residual_ref, sems.at[4]),
    ]
    copies = [
        pltpu.make_async_copy(first_hbm, first_w, sems.at[1]),
        pltpu.make_async_copy(second_hbm, second_w, sems.at[2]),
    ]
    for copy in placed + cells + copies:
        copy.start()
    for copy in placed + cells:
        copy.wait()
    for window in range(windows):
        part = slice(window * members, (window + 1) * members)
        heads = heads_ref[:, window % narrow, window // narrow]
        normed_s[part] = heads.reshape(members, channels)
    residual_s[...] = residual_ref[...] + jnp.dot(
        normed_s[...], out_w[...], preferred_element_type=jnp.float32
    )
    for window in range(windows):
        part = slice(window * members, (window + 1) * members)
        normed_s[part] = (layer_norm(residual_s[part]) * gain_ref[...]).astype(jnp.bfloat16)
    copies[0].wait()
    for start in range(0, hidden, channels):
        part = slice(start, start + channels)
        inner = jnp.dot(normed_s[...], first_w[:, part], preferred_element_type=jnp.float32)
        root = 0.7978845608028654
        angle = inner * (root + (root * 0.044715) * (inner * inner))
        halved = 0.5 * inner
        active_s[:, part] = (halved + halved * jnp.tanh(angle)).astype(jnp.bfloat16)
    copies[1].wait()
    residual_s[...] += jnp.dot(active_s[...], second_w[...], preferred_element_type=jnp.float32)
    stores = []
    for window in range(windows):
        store = pltpu.make_async_copy(
            residual_s.at[pl.ds(window * members, members)].reshape(rows, WIN, channels),
            result_hbm.at[sample, :, pl.ds(window * WIN, WIN), :],
            sems.at[0],
        )
        store.start()
        stores.append(store)
    for store in stores:
        store.wait()


VMEM = pl.BlockSpec(memory_space=pltpu.MemorySpace.VMEM)
HBM = pl.BlockSpec(memory_space=pltpu.MemorySpace.HBM)
SMEM = pl.BlockSpec(memory_space=pltpu.MemorySpace.SMEM)
PARAMS = dict(vmem_limit_bytes=48 * 1024 * 1024)


def pinned(call, *arrays):
    return call(
        *(
            pltpu.with_memory_space_constraint(a, pltpu.HBM) if a.size > 1024 else a
            for a in arrays
        )
    )


def lift_matrix(rows, cols, stride):
    def along(count):
        fine = np.arange(count)
        place = np.zeros((count, count // 2 + 2), np.float32)
        middle = fine // 2 + 1
        place[fine, middle] = 0.75
        place[fine, middle + np.where(fine % 2 == 0, -1, 1)] = 0.25
        return place

    by_row = along(rows)
    by_col = along(cols)
    by_col = np.pad(by_col, ((0, 0), (0, stride - by_col.shape[1])))
    both = by_row[:, None, :, None] * by_col[None, :, None, :]
    both = both.reshape(rows, cols // WIN, WIN, -1).transpose(1, 0, 2, 3)
    return jnp.asarray(both.reshape(rows * cols, -1), jnp.bfloat16)


def on_device(
    latent,
    context,
    conv_weight,
    window_qkv,
    window_out,
    window_bias,
    grid_qkv,
    grid_out,
    grid_bias,
    mlp_gain,
    mlp_in,
    mlp_out,
):
    samples, rows, cols, channels = latent.shape
    wide_count = lax.axis_size("wide")
    narrow = lax.axis_size("narrow")
    half_rows, half_cols, coarse = context.shape[1:]
    hidden = mlp_in.shape[1]
    members = WIN * WIN
    windows = cols // WIN
    planes = WIN // narrow
    split = wide_count // WIN
    assert rows == WIN and planes * narrow == WIN and split * WIN == wide_count
    assert windows == planes * narrow and WIN % split == 0
    stride = -(-(half_cols + 10) // 16) * 16

    low, high = neighbours(context, "wide", 1, 2)
    parts = (low, context, high)
    forward = [(i, i + 1) for i in range(narrow - 1)]
    backward = [(target, source) for source, target in forward]
    left = lax.ppermute(
        jnp.concatenate([part[:, :, half_cols - 2 :] for part in parts], axis=1), "narrow", forward
    )
    right = lax.ppermute(
        jnp.concatenate([part[:, :, :2] for part in parts], axis=1), "narrow", backward
    )
    heads_count = window_bias.shape[0]
    places = window_bias.shape[1] * window_bias.shape[2]
    flat_bias = jnp.concatenate([window_bias, grid_bias], axis=0).reshape(-1, places)
    table = jax.ShapeDtypeStruct((WIN * WIN, heads_count * WIN * WIN), jnp.float32)
    window_table, grid_table = pl.pallas_call(
        bias_kernel,
        out_shape=(table, table),
        in_specs=[VMEM, VMEM],
        out_specs=(VMEM, VMEM),
        scratch_shapes=[pltpu.VMEM((2 * heads_count * WIN, LANES), jnp.float32)],
        compiler_params=pltpu.CompilerParams(**PARAMS),
        name="bias",
    )(flat_bias, bias_pick(places))
    window_vt = window_qkv[:, 2 * channels :].T
    grid_vt = grid_qkv[:, 2 * channels :].T
    lift = lift_matrix(rows, cols, stride)
    conv_flat = conv_weight.reshape(9 * coarse, channels)
    place = jnp.stack(
        [
            lax.axis_index("wide") * half_rows - 1,
            lax.axis_index("narrow") * half_cols - 1,
            jnp.int32(wide_count * half_rows),
            jnp.int32(narrow * half_cols),
        ]
    ).astype(jnp.int32)

    bf16, f32 = jnp.bfloat16, jnp.float32
    tokens = rows * cols
    span = half_rows + 2
    def window_call(sample):
        return pl.pallas_call(
            functools.partial(window_kernel, stride=stride, sample=sample),
            out_shape=(
                pltpu.HBM((tokens, channels), f32),
                pltpu.HBM((rows, narrow, planes, WIN, channels), bf16),
            ),
            in_specs=[SMEM] + [HBM] * 12,
            out_specs=(HBM, HBM),
            scratch_shapes=[
                pltpu.VMEM((rows, cols, channels), f32),
                pltpu.VMEM((half_rows, half_cols, coarse), bf16),
                pltpu.VMEM((2, half_cols, coarse), bf16),
                pltpu.VMEM((2, half_cols, coarse), bf16),
                pltpu.VMEM((half_rows + 4, 2, coarse), bf16),
                pltpu.VMEM((half_rows + 4, 2, coarse), bf16),
                pltpu.VMEM((tokens, span * stride), bf16),
                pltpu.VMEM((members, heads_count * members), f32),
                pltpu.VMEM((9 * coarse, channels), bf16),
                pltpu.VMEM((channels, 2 * channels), bf16),
                pltpu.VMEM((channels, channels), bf16),
                pltpu.VMEM((channels, channels), bf16),
                pltpu.VMEM(((half_rows + 4) * stride + 16, coarse), f32),
                pltpu.VMEM(((half_rows + 4) * stride, 3 * coarse), bf16),
                pltpu.VMEM((span * stride, channels), bf16),
                pltpu.VMEM((tokens, channels), f32),
                pltpu.VMEM((tokens, channels), bf16),
                pltpu.VMEM((tokens, 2 * channels), bf16),
                pltpu.VMEM((heads_count // 2, 2 * HEAD + 16, tokens), bf16),
                pltpu.VMEM((2, members, heads_count * members), f32),
                pltpu.VMEM((2, 1, heads_count * members), f32),
                pltpu.VMEM((2, members, heads_count * members), bf16),
                pltpu.VMEM((tokens, channels), bf16),
                pltpu.VMEM((rows, narrow, planes, WIN, channels), bf16),
                pltpu.SemaphoreType.DMA((7,)),
                pltpu.SemaphoreType.DMA((2,)),
            ],
            compiler_params=pltpu.CompilerParams(**PARAMS),
            name="window",
        )

    grid_call = pl.pallas_call(
        grid_kernel,
        out_shape=pltpu.HBM((tokens, channels), bf16),
        in_specs=[HBM] * 4,
        out_specs=HBM,
        scratch_shapes=[
            pltpu.VMEM((tokens, channels), bf16),
            pltpu.VMEM((channels, 2 * channels), bf16),
            pltpu.VMEM((channels, channels), bf16),
            pltpu.VMEM((channels // LANES, tokens, LANES), f32),
            pltpu.VMEM((tokens, channels), bf16),
            pltpu.VMEM((tokens, 2 * channels), bf16),
            pltpu.VMEM((heads_count // 2, 2 * HEAD + 16, tokens), bf16),
            pltpu.VMEM((2, members, heads_count * members), f32),
            pltpu.VMEM((2, 1, heads_count * members), f32),
            pltpu.VMEM((2, members, heads_count * members), bf16),
            pltpu.VMEM((members, heads_count * members), f32),
            pltpu.SemaphoreType.DMA((4,)),
        ],
        compiler_params=pltpu.CompilerParams(**PARAMS),
        name="grid",
    )

    def mlp_call(sample):
        first = sample == 0
        return pl.pallas_call(
            functools.partial(mlp_kernel, sample=sample),
            out_shape=pltpu.HBM((samples, rows, cols, channels), f32),
            in_specs=[HBM, HBM, VMEM] + [HBM] * (3 if first else 4),
            out_specs=HBM,
            input_output_aliases={} if first else {6: 0},
            scratch_shapes=[
                pltpu.VMEM((tokens, channels), f32),
                pltpu.VMEM((rows, narrow, planes, WIN, channels), bf16),
                pltpu.VMEM((channels, channels), bf16),
                pltpu.VMEM((channels, hidden), bf16),
                pltpu.VMEM((hidden, channels), bf16),
                pltpu.VMEM((tokens, channels), f32),
                pltpu.VMEM((tokens, channels), bf16),
                pltpu.VMEM((tokens, hidden), bf16),
                pltpu.SemaphoreType.DMA((5,)),
            ],
            compiler_params=pltpu.CompilerParams(**PARAMS),
            name="mlp",
        )

    gain = mlp_gain.reshape(1, channels)

    def send(normed):
        pieces = normed.reshape(rows, narrow, planes, split, WIN // split, channels)
        pieces = pieces.transpose(0, 3, 1, 2, 4, 5)
        pieces = pieces.reshape(wide_count * narrow, planes, WIN // split, channels)
        received = lax.all_to_all(pieces, JOINT, split_axis=0, concat_axis=0, tiled=True)
        received = received.reshape(WIN, split, narrow, planes, WIN // split, channels)
        return received.transpose(0, 2, 3, 1, 4, 5).reshape(tokens, channels)

    def send_back(heads):
        pieces = heads.reshape(WIN, narrow, planes, split, WIN // split, channels)
        pieces = pieces.transpose(0, 3, 1, 2, 4, 5)
        pieces = pieces.reshape(wide_count * narrow, planes, WIN // split, channels)
        received = lax.all_to_all(pieces, JOINT, split_axis=0, concat_axis=0, tiled=True)
        received = received.reshape(rows, split, narrow, planes, WIN // split, channels)
        return received.transpose(0, 2, 3, 1, 4, 5).reshape(rows, narrow, planes, WIN, channels)

    residuals, cells = [], []
    for sample in range(samples):
        residual, normed = pinned(
            window_call(sample),
            place,
            latent,
            context,
            low,
            high,
            left,
            right,
            lift,
            window_table,
            conv_flat,
            window_qkv,
            window_vt,
            window_out,
        )
        residuals.append(residual)
        cells.append(send(normed))
    returned = []
    for sample in range(samples):
        heads = pinned(grid_call, cells[sample], grid_table, grid_qkv, grid_vt)
        returned.append(send_back(heads))
    result = ()
    for sample in range(samples):
        result = (
            pinned(
                mlp_call(sample), residuals[sample], returned[sample], gain, grid_out, mlp_in, mlp_out, *result
            ),
        )
    return result[0]


def solution(mesh):
    return jax.shard_map(
        on_device,
        mesh=mesh,
        in_specs=(
            P(None, "wide", "narrow", None),
            P(None, "wide", "narrow", None),
        )
        + (P(),) * 10,
        out_specs=P(None, "wide", "narrow", None),
        check_vma=False,
    )
```

```python
import functools
import math

import jax
import jax.numpy as jnp
import numpy as np
from jax import lax
from jax.experimental import pallas as pl
from jax.experimental.pallas import tpu as pltpu
from jax.sharding import PartitionSpec as P

HEAD = 32
WIN = 8
NORM_EPS = 1e-05
LANES = 128
HALVES = 2
LOG2E = math.log2(math.e)
JOINT = ("wide", "narrow")


def neighbours(first, last, axis):
    count = lax.axis_size(axis)
    rounds = [
        [pair for i in range(start, count - 1, 2) for pair in ((i, i + 1), (i + 1, i))]
        for start in (0, 1)
    ]
    odd = lax.axis_index(axis) % 2 == 1
    inner = lax.ppermute(jnp.where(odd, first, last), axis, rounds[0])
    outer = lax.ppermute(jnp.where(odd, last, first), axis, rounds[1])
    return jnp.where(odd, inner, outer), jnp.where(odd, outer, inner)


def prepare_kernel(flat_ref, conv_hbm, window_ref, grid_ref, conv_ref, spread_s, sem):
    conv_copy = pltpu.make_async_copy(conv_hbm, conv_ref, sem)
    conv_copy.start()
    both, places = flat_ref.shape
    side = WIN
    flat = flat_ref[...] * LOG2E
    top = flat.astype(jnp.bfloat16)
    rest = flat - top.astype(jnp.float32)
    middle = rest.astype(jnp.bfloat16)
    last = (rest - middle.astype(jnp.float32)).astype(jnp.bfloat16)
    stacked = jnp.concatenate([top, middle, last], axis=0)
    span = 2 * side - 1
    place = lax.broadcasted_iota(jnp.int32, (places, LANES), 0)
    lane = lax.broadcasted_iota(jnp.int32, (places, LANES), 1)
    ahead = place - (lane // side) * span - lane % side - (side - 1)
    for key_col in range(side):
        pick = jnp.where(ahead == -key_col, 1.0, 0.0).astype(jnp.bfloat16)
        picked = jnp.dot(stacked, pick, preferred_element_type=jnp.float32)
        spread_s[pl.ds(key_col, both, stride=side), :] = (
            picked[:both] + picked[both : 2 * both]
        ) + picked[2 * both :]
    low_half = lax.broadcasted_iota(jnp.int32, (side, LANES), 1) < side * side
    heads = both // 2
    for table, table_ref in enumerate((window_ref, grid_ref)):
        for pair in range(heads // 2):
            base = (table * heads + 2 * pair) * side
            even = spread_s[base : base + side]
            odd = spread_s[base + side : base + 2 * side]
            for key_row in range(side):
                start = side * (side - 1 - key_row)
                even_part = pltpu.roll(even, (LANES - start) % LANES, 1)
                odd_part = pltpu.roll(odd, (LANES - start + side * side) % LANES, 1)
                table_ref[
                    key_row * side : (key_row + 1) * side, pair * LANES : (pair + 1) * LANES
                ] = jnp.where(low_half, even_part, odd_part)
    conv_copy.wait()


def layer_norm(values):
    center = values - jnp.mean(values, axis=-1, keepdims=True)
    spread = jnp.mean(center * center, axis=-1, keepdims=True)
    return center * lax.rsqrt(spread + NORM_EPS)


def project(normed_s, qkv_w, qk_s, vt_s, wait):
    channels = normed_s.shape[1]
    wait.wait()
    queries = jnp.dot(
        normed_s[...], qkv_w[:, :channels], preferred_element_type=jnp.float32
    )
    qk_s[:, :channels] = (queries * (LOG2E * HEAD ** (-0.5))).astype(jnp.bfloat16)
    qk_s[:, channels:] = jnp.dot(
        normed_s[...], qkv_w[:, channels : 2 * channels], preferred_element_type=jnp.float32
    ).astype(jnp.bfloat16)
    values = jnp.dot(
        normed_s[...], qkv_w[:, 2 * channels :], preferred_element_type=jnp.float32
    )
    values = values.T.astype(jnp.bfloat16)
    pairs, tall = vt_s.shape[:2]
    for pair in range(pairs):
        vt_s[pair, : 2 * HEAD] = values[pair * 2 * HEAD : (pair + 1) * 2 * HEAD]
        vt_s[pair, 2 * HEAD :] = jnp.ones((tall - 2 * HEAD, values.shape[1]), jnp.bfloat16)


def attend(groups, qk_s, vt_s, bias_s, score_s, top_s, lifted_s, store):
    members = WIN * WIN
    channels = qk_s.shape[1] // 2
    blocks = channels // LANES
    per = LANES // HEAD
    wide = per * members
    lane_head = lax.broadcasted_iota(jnp.int32, (members, LANES), 1) // HEAD
    own = [lane_head == h for h in range(per)]
    low_half = lax.broadcasted_iota(jnp.int32, (HEAD, LANES), 1) < members

    def scores(group, block):
        rows = slice(group * members, (group + 1) * members)
        part = slice(block * wide, (block + 1) * wide)
        queries = qk_s[rows, block * LANES : (block + 1) * LANES]
        keys = qk_s[rows, channels + block * LANES : channels + (block + 1) * LANES]
        zero = jnp.zeros_like(queries)
        spread = jnp.concatenate([jnp.where(mask, queries, zero) for mask in own], axis=0)
        score = lax.dot_general(
            keys, spread, (((1,), (1,)), ((), ())), preferred_element_type=jnp.float32
        )
        score = score + bias_s[:, part]
        score_s[group % 2, :, part] = score
        top_s[group % 2, :, part] = jnp.max(score, axis=0, keepdims=True)

    def lift(group, block):
        part = slice(block * wide, (block + 1) * wide)
        lifted = jnp.exp2(score_s[group % 2, :, part] - top_s[group % 2, :, part])
        lifted_s[group % 2, :, part] = lifted.astype(jnp.bfloat16)

    def blend(group, block):
        pieces = []
        for pair in range(block * per // 2, (block + 1) * per // 2):
            values = vt_s[pair, :, group * members : (group + 1) * members]
            mixed = jnp.dot(
                values,
                lifted_s[group % 2, :, pair * LANES : (pair + 1) * LANES],
                preferred_element_type=jnp.float32,
            )
            chosen = jnp.where(low_half, mixed[:HEAD], mixed[HEAD : 2 * HEAD])
            pieces.append(chosen * (1.0 / mixed[2 * HEAD : 2 * HEAD + 1]))
        return pieces

    for step in range(groups + 2):
        pieces = []
        for block in range(blocks):
            if step < groups:
                scores(step, block)
            if 0 <= step - 1 < groups:
                lift(step - 1, block)
            if step >= 2:
                pieces.extend(blend(step - 2, block))
        if pieces:
            turned = jnp.concatenate(pieces, axis=0).T
            store(step - 2, jnp.concatenate([turned[:members], turned[members:]], axis=1))


def out_copies(weight_ref, buffer_ref, sem):
    pairs = weight_ref.shape[0] // (2 * HEAD)
    return [
        pltpu.make_async_copy(
            weight_ref.at[pl.ds((2 * pair + parity) * HEAD, HEAD)],
            buffer_ref.at[pl.ds((parity * pairs + pair) * HEAD, HEAD)],
            sem,
        )
        for parity in range(2)
        for pair in range(pairs)
    ]


def window_kernel(
    place_ref,
    low_ref,
    high_ref,
    left_ref,
    right_ref,
    bias_s,
    conv_w,
    context_hbm,
    latent_hbm,
    lift_hbm,
    qkv_hbm,
    out_hbm,
    residual_hbm,
    normed_hbm,
    latent_ref,
    context_ref,
    lift_ref,
    qkv_w,
    out_w,
    wide_s,
    taps_s,
    features_s,
    residual_ref,
    normed_s,
    qk_s,
    vt_s,
    score_s,
    top_s,
    lifted_s,
    heads_s,
    sent_s,
    sems,
    out_sems,
    *,
    stride,
    sample,
):
    rows, cols, channels = latent_ref.shape
    half_rows, half_cols, coarse = context_ref.shape
    members = WIN * WIN
    windows = cols // WIN
    context_copy = pltpu.make_async_copy(context_hbm.at[sample], context_ref, sems.at[0])
    cells_copies = [
        pltpu.make_async_copy(lift_hbm, lift_ref, sems.at[1]),
        pltpu.make_async_copy(latent_hbm.at[sample], latent_ref, sems.at[1]),
    ]
    qkv_copy = pltpu.make_async_copy(qkv_hbm, qkv_w, sems.at[2])
    placed = out_copies(out_hbm, out_w, sems.at[3])
    for copy in [context_copy] + cells_copies + [qkv_copy] + placed:
        copy.start()
    span = half_rows + 2
    context_copy.wait()
    for row in range(half_rows + 4):
        base = row * stride
        if row < 2:
            middle = low_ref[sample, row]
        elif row < half_rows + 2:
            middle = context_ref[row - 2]
        else:
            middle = high_ref[sample, row - half_rows - 2]
        wide_s[base + 6 : base + 8] = left_ref[sample, row].astype(jnp.float32)
        wide_s[base + 8 : base + 8 + half_cols] = middle.astype(jnp.float32)
        wide_s[base + 8 + half_cols : base + 10 + half_cols] = right_ref[sample, row].astype(jnp.float32)
    tall = (half_rows + 4) * stride
    for shift in range(3):
        taps_s[:, shift * coarse : (shift + 1) * coarse] = wide_s[
            shift + 6 : shift + 6 + tall
        ].astype(jnp.bfloat16)
    patches = jnp.concatenate(
        [taps_s[shift * stride : (shift + span) * stride] for shift in range(3)], axis=1
    )
    total = jnp.dot(patches, conv_w[...], preferred_element_type=jnp.float32)
    column = lax.broadcasted_iota(jnp.int32, (stride, channels), 0)
    col_place = column + place_ref[1]
    col_inside = (col_place >= 0) & (col_place < place_ref[3]) & (column < half_cols + 2)
    for row in range(span):
        row_place = place_ref[0] + row
        inside = col_inside & ((row_place >= 0) & (row_place < place_ref[2]))
        part = slice(row * stride, (row + 1) * stride)
        features_s[part] = jnp.where(inside, total[part], 0.0).astype(jnp.bfloat16)

    for copy in cells_copies:
        copy.wait()
    residual_ref[...] = jnp.dot(
        lift_ref[...], features_s[...], preferred_element_type=jnp.float32
    )
    for window in range(windows):
        part = slice(window * members, (window + 1) * members)
        cells = latent_ref[:, window * WIN : (window + 1) * WIN, :].reshape(members, channels)
        residual = cells + residual_ref[part]
        residual_ref[part] = residual
        normed_s[part] = layer_norm(residual).astype(jnp.bfloat16)

    project(normed_s, qkv_w, qk_s, vt_s, qkv_copy)

    def store_heads(window, heads):
        heads_s[window * members : (window + 1) * members] = heads.astype(jnp.bfloat16)

    attend(windows, qk_s, vt_s, bias_s, score_s, top_s, lifted_s, store_heads)
    for copy in placed:
        copy.wait()
    residual_ref[...] += jnp.dot(heads_s[...], out_w[...], preferred_element_type=jnp.float32)
    narrow = normed_hbm.shape[1]
    for window in range(windows):
        part = slice(window * members, (window + 1) * members)
        normed = layer_norm(residual_ref[part]).astype(jnp.bfloat16)
        sent_s[:, window % narrow, window // narrow] = normed.reshape(rows, WIN, channels)
    stores = [
        pltpu.make_async_copy(sent_s, normed_hbm, out_sems.at[0]),
        pltpu.make_async_copy(residual_ref, residual_hbm, out_sems.at[1]),
    ]
    for store in stores:
        store.start()
    for store in stores:
        store.wait()


def grid_kernel(
    cells_hbm,
    bias_hbm,
    qkv_hbm,
    heads_hbm,
    cells_ref,
    qkv_w,
    spread_s,
    normed_s,
    qk_s,
    vt_s,
    score_s,
    top_s,
    lifted_s,
    bias_s,
    sems,
):
    tokens, channels = cells_ref.shape
    groups = WIN
    members = tokens // groups
    copies = [
        pltpu.make_async_copy(cells_hbm, cells_ref, sems.at[0]),
        pltpu.make_async_copy(qkv_hbm, qkv_w, sems.at[1]),
        pltpu.make_async_copy(bias_hbm, bias_s, sems.at[2]),
    ]
    for copy in copies:
        copy.start()
    copies[0].wait()
    lanes = [slice(start, start + LANES) for start in range(0, channels, LANES)]
    for chunk, lane in enumerate(lanes):
        spread_s[chunk] = cells_ref[:, lane].astype(jnp.float32)
    for group in range(groups):
        for chunk, lane in enumerate(lanes):
            normed_s[group * members : (group + 1) * members, lane] = spread_s[
                chunk, pl.ds(group, members, stride=groups), :
            ].astype(jnp.bfloat16)
    project(normed_s, qkv_w, qk_s, vt_s, copies[1])
    copies[2].wait()

    def store_heads(group, heads):
        for chunk, lane in enumerate(lanes):
            spread_s[chunk, pl.ds(group, members, stride=groups), :] = heads[:, lane]

    attend(groups, qk_s, vt_s, bias_s, score_s, top_s, lifted_s, store_heads)
    for chunk, lane in enumerate(lanes):
        cells_ref[:, lane] = spread_s[chunk].astype(jnp.bfloat16)
    store = pltpu.make_async_copy(cells_ref, heads_hbm, sems.at[0])
    store.start()
    store.wait()


def mlp_kernel(
    *refs,
    sample,
):
    (
        residual_hbm,
        heads_hbm,
        gain_ref,
        out_hbm,
        first_hbm,
        second_hbm,
    ) = refs[:6]
    (
        result_hbm,
        residual_ref,
        heads_ref,
        out_w,
        first_w,
        second_w,
        residual_s,
        normed_s,
        active_s,
        sems,
    ) = refs[-10:]
    tokens, channels = residual_ref.shape
    members = WIN * WIN
    windows = tokens // members
    rows, narrow = heads_ref.shape[:2]
    hidden = first_w.shape[1]
    placed = out_copies(out_hbm, out_w, sems.at[0])
    cells = [
        pltpu.make_async_copy(heads_hbm, heads_ref, sems.at[3]),
        pltpu.make_async_copy(residual_hbm, residual_ref, sems.at[4]),
    ]
    copies = [
        pltpu.make_async_copy(first_hbm, first_w, sems.at[1]),
        pltpu.make_async_copy(second_hbm, second_w, sems.at[2]),
    ]
    for copy in cells[:1] + placed + cells[1:] + copies:
        copy.start()
    cells[0].wait()
    for window in range(windows):
        part = slice(window * members, (window + 1) * members)
        heads = heads_ref[:, window % narrow, window // narrow]
        normed_s[part] = heads.reshape(members, channels)
    for copy in placed + cells[1:]:
        copy.wait()
    residual_s[...] = residual_ref[...] + jnp.dot(
        normed_s[...], out_w[...], preferred_element_type=jnp.float32
    )
    for window in range(windows):
        part = slice(window * members, (window + 1) * members)
        normed_s[part] = (layer_norm(residual_s[part]) * gain_ref[...]).astype(jnp.bfloat16)
    for copy in copies:
        copy.wait()
    stores = []
    span = tokens // HALVES
    for half in range(HALVES):
        rows_in = slice(half * span, (half + 1) * span)
        for start in range(0, hidden, channels):
            part = slice(start, start + channels)
            inner = jnp.dot(
                normed_s[rows_in], first_w[:, part], preferred_element_type=jnp.float32
            )
            root = 0.7978845608028654
            angle = inner * (root + (root * 0.044715) * (inner * inner))
            active_s[half, :, part] = (inner * (1.0 + jnp.tanh(angle))).astype(jnp.bfloat16)
        doubled = jnp.dot(active_s[half], second_w[...], preferred_element_type=jnp.float32)
        residual_s[rows_in] = residual_s[rows_in] + 0.5 * doubled
        for window in range(half * windows // HALVES, (half + 1) * windows // HALVES):
            store = pltpu.make_async_copy(
                residual_s.at[pl.ds(window * members, members)].reshape(rows, WIN, channels),
                result_hbm.at[sample, :, pl.ds(window * WIN, WIN), :],
                sems.at[0],
            )
            store.start()
            stores.append(store)
    for store in stores:
        store.wait()


VMEM = pl.BlockSpec(memory_space=pltpu.MemorySpace.VMEM)
ANY = pl.BlockSpec(memory_space=pl.ANY)
HBM = pl.BlockSpec(memory_space=pltpu.MemorySpace.HBM)
SMEM = pl.BlockSpec(memory_space=pltpu.MemorySpace.SMEM)
PARAMS = dict(vmem_limit_bytes=48 * 1024 * 1024)


def in_hbm(*arrays):
    return [pltpu.with_memory_space_constraint(array, pltpu.HBM) for array in arrays]


def lift_matrix(rows, cols, stride):
    def along(count):
        fine = np.arange(count)
        place = np.zeros((count, count // 2 + 2), np.float32)
        middle = fine // 2 + 1
        place[fine, middle] = 0.75
        place[fine, middle + np.where(fine % 2 == 0, -1, 1)] = 0.25
        return place

    by_row = along(rows)
    by_col = along(cols)
    by_col = np.pad(by_col, ((0, 0), (0, stride - by_col.shape[1])))
    both = by_row[:, None, :, None] * by_col[None, :, None, :]
    both = both.reshape(rows, cols // WIN, WIN, -1).transpose(1, 0, 2, 3)
    return jnp.asarray(both.reshape(rows * cols, -1), jnp.bfloat16)


def on_device(
    latent,
    context,
    conv_weight,
    window_qkv,
    window_out,
    window_bias,
    grid_qkv,
    grid_out,
    grid_bias,
    mlp_gain,
    mlp_in,
    mlp_out,
):
    samples, rows, cols, channels = latent.shape
    wide_count = lax.axis_size("wide")
    narrow = lax.axis_size("narrow")
    half_rows, half_cols, coarse = context.shape[1:]
    hidden = mlp_in.shape[1]
    members = WIN * WIN
    windows = cols // WIN
    planes = WIN // narrow
    split = wide_count // WIN
    assert rows == WIN and planes * narrow == WIN and split * WIN == wide_count
    assert windows == planes * narrow and WIN % split == 0
    stride = -(-(half_cols + 10) // 16) * 16

    low, high = neighbours(context[:, :2], context[:, half_rows - 2 :], "wide")
    parts = (low, context, high)
    left, right = neighbours(
        jnp.concatenate([part[:, :, :2] for part in parts], axis=1),
        jnp.concatenate([part[:, :, half_cols - 2 :] for part in parts], axis=1),
        "narrow",
    )
    heads_count = window_bias.shape[0]
    places = window_bias.shape[1] * window_bias.shape[2]
    flat_bias = jnp.concatenate([window_bias, grid_bias], axis=0).reshape(-1, places)
    table = jax.ShapeDtypeStruct((WIN * WIN, heads_count * WIN * WIN), jnp.float32)
    conv_flat = conv_weight.reshape(9 * coarse, channels)
    window_table, grid_table, conv_near = pl.pallas_call(
        prepare_kernel,
        out_shape=(table, table, jax.ShapeDtypeStruct(conv_flat.shape, conv_flat.dtype)),
        in_specs=[VMEM, HBM],
        out_specs=(VMEM, VMEM, VMEM),
        scratch_shapes=[
            pltpu.VMEM((2 * heads_count * WIN, LANES), jnp.float32),
            pltpu.SemaphoreType.DMA,
        ],
        compiler_params=pltpu.CompilerParams(**PARAMS),
        name="prepare",
    )(flat_bias, *in_hbm(conv_flat))
    lift = lift_matrix(rows, cols, stride)
    place = jnp.stack(
        [
            lax.axis_index("wide") * half_rows - 1,
            lax.axis_index("narrow") * half_cols - 1,
            jnp.int32(wide_count * half_rows),
            jnp.int32(narrow * half_cols),
        ]
    ).astype(jnp.int32)

    bf16, f32 = jnp.bfloat16, jnp.float32
    tokens = rows * cols
    span = half_rows + 2
    def window_call(sample):
        return pl.pallas_call(
            functools.partial(window_kernel, stride=stride, sample=sample),
            out_shape=(
                pltpu.HBM((tokens, channels), f32),
                pltpu.HBM((rows, narrow, planes, WIN, channels), bf16),
            ),
            in_specs=[SMEM] + [VMEM] * 6 + [HBM] * 5,
            out_specs=(HBM, HBM),
            scratch_shapes=[
                pltpu.VMEM((rows, cols, channels), f32),
                pltpu.VMEM((half_rows, half_cols, coarse), bf16),
                pltpu.VMEM((tokens, span * stride), bf16),
                pltpu.VMEM((channels, 3 * channels), bf16),
                pltpu.VMEM((channels, channels), bf16),
                pltpu.VMEM(((half_rows + 4) * stride + 16, coarse), f32),
                pltpu.VMEM(((half_rows + 4) * stride, 3 * coarse), bf16),
                pltpu.VMEM((span * stride, channels), bf16),
                pltpu.VMEM((tokens, channels), f32),
                pltpu.VMEM((tokens, channels), bf16),
                pltpu.VMEM((tokens, 2 * channels), bf16),
                pltpu.VMEM((heads_count // 2, 2 * HEAD + 16, tokens), bf16),
                pltpu.VMEM((2, members, heads_count * members), f32),
                pltpu.VMEM((2, 1, heads_count * members), f32),
                pltpu.VMEM((2, members, heads_count * members), bf16),
                pltpu.VMEM((tokens, channels), bf16),
                pltpu.VMEM((rows, narrow, planes, WIN, channels), bf16),
                pltpu.SemaphoreType.DMA((4,)),
                pltpu.SemaphoreType.DMA((2,)),
            ],
            compiler_params=pltpu.CompilerParams(**PARAMS),
            name="window",
        )

    grid_call = pl.pallas_call(
        grid_kernel,
        out_shape=pltpu.HBM((tokens, channels), bf16),
        in_specs=[ANY] + [HBM] * 2,
        out_specs=HBM,
        scratch_shapes=[
            pltpu.VMEM((tokens, channels), bf16),
            pltpu.VMEM((channels, 3 * channels), bf16),
            pltpu.VMEM((channels // LANES, tokens, LANES), f32),
            pltpu.VMEM((tokens, channels), bf16),
            pltpu.VMEM((tokens, 2 * channels), bf16),
            pltpu.VMEM((heads_count // 2, 2 * HEAD + 16, tokens), bf16),
            pltpu.VMEM((2, members, heads_count * members), f32),
            pltpu.VMEM((2, 1, heads_count * members), f32),
            pltpu.VMEM((2, members, heads_count * members), bf16),
            pltpu.VMEM((members, heads_count * members), f32),
            pltpu.SemaphoreType.DMA((3,)),
        ],
        compiler_params=pltpu.CompilerParams(**PARAMS),
        name="grid",
    )

    def mlp_call(sample):
        first = sample == 0
        return pl.pallas_call(
            functools.partial(mlp_kernel, sample=sample),
            out_shape=pltpu.HBM((samples, rows, cols, channels), f32),
            in_specs=[HBM, ANY, VMEM] + [HBM] * (3 if first else 4),
            out_specs=HBM,
            input_output_aliases={} if first else {6: 0},
            scratch_shapes=[
                pltpu.VMEM((tokens, channels), f32),
                pltpu.VMEM((rows, narrow, planes, WIN, channels), bf16),
                pltpu.VMEM((channels, channels), bf16),
                pltpu.VMEM((channels, hidden), bf16),
                pltpu.VMEM((hidden, channels), bf16),
                pltpu.VMEM((tokens, channels), f32),
                pltpu.VMEM((tokens, channels), bf16),
                pltpu.VMEM((HALVES, tokens // HALVES, hidden), bf16),
                pltpu.SemaphoreType.DMA((5,)),
            ],
            compiler_params=pltpu.CompilerParams(**PARAMS),
            name="mlp",
        )

    context, latent, lift, window_qkv, window_out = in_hbm(
        context, latent, lift, window_qkv, window_out
    )
    grid_table, grid_qkv, grid_out, mlp_in, mlp_out = in_hbm(
        grid_table, grid_qkv, grid_out, mlp_in, mlp_out
    )
    gain = mlp_gain.reshape(1, channels)

    def send(normed):
        pieces = normed.reshape(rows, narrow, planes, split, WIN // split, channels)
        pieces = pieces.transpose(0, 3, 1, 2, 4, 5)
        pieces = pieces.reshape(wide_count * narrow, planes, WIN // split, channels)
        received = lax.all_to_all(pieces, JOINT, split_axis=0, concat_axis=0, tiled=True)
        received = received.reshape(WIN, split, narrow, planes, WIN // split, channels)
        return received.transpose(0, 2, 3, 1, 4, 5).reshape(tokens, channels)

    def send_back(heads):
        pieces = heads.reshape(WIN, narrow, planes, split, WIN // split, channels)
        pieces = pieces.transpose(0, 3, 1, 2, 4, 5)
        pieces = pieces.reshape(wide_count * narrow, planes, WIN // split, channels)
        received = lax.all_to_all(pieces, JOINT, split_axis=0, concat_axis=0, tiled=True)
        received = received.reshape(rows, split, narrow, planes, WIN // split, channels)
        return received.transpose(0, 2, 3, 1, 4, 5).reshape(rows, narrow, planes, WIN, channels)

    residuals, cells = [], []
    for sample in range(samples):
        residual, normed = window_call(sample)(
            place,
            low,
            high,
            left,
            right,
            window_table,
            conv_near,
            context,
            latent,
            lift,
            window_qkv,
            window_out,
        )
        residuals.append(residual)
        cells.append(send(normed))
    returned = []
    for sample in range(samples):
        heads = grid_call(cells[sample], grid_table, grid_qkv)
        returned.append(send_back(heads))
    result = ()
    for sample in range(samples):
        result = (
            mlp_call(sample)(
                residuals[sample], returned[sample], gain, grid_out, mlp_in, mlp_out, *result
            ),
        )
    return result[0]


def solution(mesh):
    return jax.shard_map(
        on_device,
        mesh=mesh,
        in_specs=(
            P(None, "wide", "narrow", None),
            P(None, "wide", "narrow", None),
        )
        + (P(),) * 10,
        out_specs=P(None, "wide", "narrow", None),
        check_vma=False,
    )
```
